256 devices in a mesh: row: 8 (over z_hi, core), col: 32 (over y, x, z_lo).
Axes of the slice: x: 4, y: 4, z: 8 (z_hi: 4, z_lo: 2; z = z_hi * 2 + z_lo), core: 2. Of those that a mesh axis runs over, the one named last changes fastest.
Arguments:
- features: bfloat16 [65536, 256], P(('row', 'col')), may hold values from -6 to 6
- layer_weight: bfloat16 [256, 256], replicated, may hold values from -0.375 to 0.375
- layer_bias: float32 [256], replicated, may hold values from -3 to 3
- cotangent: bfloat16 [65536, 256], P(('row', 'col')), may hold values from -6 to 6
- tile_values: bfloat16 [8192, 256, 256], P(('row', 'col')), may hold values from -0.0625 to 0.0625
- tile_index: int32 [8192, 2], P(('row', 'col')), may hold values from -1 to 255, as said below
Outputs:
- activations: bfloat16 [65536, 256], P(('row', 'col'))
- node_grad: bfloat16 [65536, 256], P(('row', 'col'))
- weight_grad: float32 [256, 256], P(('row', 'col'))
- bias_grad: float32 [256], P(('row', 'col'))
The draws below stay inside these ranges and needn't reach their ends.
Inputs may be any that keep to these rules, and one draw needn't show every extreme that they name: `tile_index`: each pair is (I, J) with I <= J; device r * 32 + c holds only pairs whose I lies in blocks r * 32 * 1 to (r + 1) * 32 - 1 and whose J // 1 equals c modulo 32. Each pair is held by at most one slot among all devices. A device's live slots come first, its empty slots hold -1 in both entries; counts differ from device to device, and some device fills all 32 slots.
All inputs are finite; a program needn't handle non-finite values.
Results may differ from the reference program's by a relative error of at most 0.025.
Values may be sent and summed in bfloat16 or wider, within the bound.
No kernel may reach another device: no remote copies, remote signals or barrier semaphores. Data moves between devices by JAX's collectives and lax.ppermute only.
A program may use at most 128 MiB of HBM per device.

```python
import jax
import jax.numpy as jnp
from jax import lax

TILE = 256
F = 256
BLK_DEV = 1
MAXT = 32
NBLK = 256
NODES = 65536
N_ROW = 8
N_COL = 32
DEVICES = 256


def draw_tile_index(key, part):
    row_devices = N_ROW
    column_devices = N_COL
    devices = row_devices * column_devices
    row_span = column_devices * BLK_DEV
    column_span = row_devices * BLK_DEV
    domain = row_span * column_span
    key_order = jax.random.fold_in(key, 11)
    key_count = jax.random.fold_in(key, 23)
    device_ids = jnp.arange(devices, dtype=jnp.int32)
    row_of = device_ids // column_devices
    column_of = device_ids % column_devices
    positions = jnp.arange(domain, dtype=jnp.int32)
    row_pos = positions // column_span
    column_pos = positions % column_span
    block_row = row_of[:, None] * row_span + row_pos[None, :]
    block_column = (column_pos[None, :] // BLK_DEV * column_devices + column_of[:, None]) * BLK_DEV + column_pos[None, :] % BLK_DEV
    allowed = (block_row <= block_column).astype(jnp.int32)
    scores = jax.random.randint(key_order, (devices, domain), 0, domain, dtype=jnp.int32) * domain + positions[None, :]
    scores = scores + allowed * (domain * domain)
    _, chosen = lax.top_k(scores, MAXT)
    allowed_count = jnp.sum(allowed, axis=1)
    wanted = jax.random.randint(key_count, (devices,), 1, MAXT + 1, dtype=jnp.int32)
    wanted = jnp.where(device_ids == column_devices - 1, MAXT, wanted)
    counts = jnp.minimum(wanted, allowed_count)
    slot_ids = jnp.arange(MAXT, dtype=jnp.int32)
    occupied = slot_ids[None, :] < counts[:, None]
    chosen_rows = jnp.take_along_axis(block_row, chosen, axis=1)
    chosen_columns = jnp.take_along_axis(block_column, chosen, axis=1)
    first = jnp.where(occupied, chosen_rows, -1)
    second = jnp.where(occupied, chosen_columns, -1)
    return jnp.stack([first, second], axis=-1).reshape(devices * MAXT, 2).astype(jnp.int32)


def block_scale(own_key, extent, shards, least, largest):
    def one(axis_at, shards_of):
        heights = jax.random.uniform(jax.random.fold_in(jax.random.fold_in(own_key, 6), axis_at), (shards_of,), jnp.float32, least / len(shards), largest / len(shards))
        return jnp.repeat(jnp.exp(heights), extent[axis_at] // shards_of).reshape((-1,) + (1,) * (len(extent) - axis_at - 1))

    level = one(*shards[0])
    for cut in shards[1:]:
        level = level * one(*cut)
    return level


def normal_values(key, extent, deviation, limit, split=(), kind=jnp.bfloat16):
    values = jax.random.normal(key, extent, jnp.float32) * deviation
    if len(split) > 0:
        values = block_scale(key, extent, split, -0.22, 0.18) * values
    return jnp.clip(values, min=-limit, max=limit).astype(kind)


def setup_inputs(seed: int = 0) -> dict:
    streams_of = jax.random.split(jax.random.key(seed), 7)
    return {
        "features": normal_values(streams_of[0], (NODES, F), 1.0, 6.0, ((0, 256),)),
        "layer_weight": normal_values(streams_of[1], (F, F), F ** -0.5, 0.375),
        "layer_bias": normal_values(streams_of[2], (F,), 0.5, 3.0, (), jnp.float32),
        "cotangent": normal_values(streams_of[3], (NODES, F), 1.0, 6.0, ((0, 256),)),
        "tile_values": normal_values(streams_of[4], (DEVICES * MAXT, TILE, TILE), (TILE * MAXT) ** -0.5, 0.0625, ((0, 256),)),
        "tile_index": draw_tile_index(jax.random.fold_in(streams_of[6], 71), 0),
    }


def aggregate(node_data, tile_values, tile_index):
    row_devices = N_ROW
    column_devices = N_COL
    feature_count = node_data.shape[1]
    row_span = column_devices * BLK_DEV
    column_span = row_devices * BLK_DEV
    blocks = node_data.reshape(NBLK, TILE, feature_count).astype(jnp.float32)
    device_tiles = tile_values.reshape(row_devices * column_devices, MAXT, TILE, TILE)
    device_slots = tile_index.reshape(row_devices * column_devices, MAXT, 2)
    device_ids = jnp.arange(row_devices * column_devices, dtype=jnp.int32)

    def visit_device(running, scan_item):
        row_total, column_total = running
        tile_block, slot_index, device = scan_item
        row_index = device // column_devices
        column_index = device % column_devices
        block_row = slot_index[:, 0]
        block_column = slot_index[:, 1]
        occupied = block_row >= 0
        forward_inputs = blocks[jnp.maximum(block_column, 0)]
        mirror_inputs = blocks[jnp.maximum(block_row, 0)]
        tile_floats = tile_block.astype(jnp.float32)
        forward_terms = jnp.einsum("tnm,tmf->tnf", tile_floats, forward_inputs, precision=lax.Precision.HIGHEST)
        mirror_terms = jnp.einsum("tmn,tmf->tnf", tile_floats, mirror_inputs, precision=lax.Precision.HIGHEST)
        row_slot = jnp.where(occupied, block_row - row_index * row_span, -1)
        column_slot = jnp.where(occupied, (block_column // BLK_DEV // column_devices) * BLK_DEV + block_column % BLK_DEV, -1)
        row_select = (row_slot[:, None] == jnp.arange(row_span, dtype=jnp.int32)[None, :]).astype(jnp.float32)
        column_select = (column_slot[:, None] == jnp.arange(column_span, dtype=jnp.int32)[None, :]).astype(jnp.float32)
        row_partial = jnp.einsum("ta,tnf->anf", row_select, forward_terms, precision=lax.Precision.HIGHEST)
        column_partial = jnp.einsum("tb,tnf->bnf", column_select, mirror_terms, precision=lax.Precision.HIGHEST)
        row_partial = lax.optimization_barrier(row_partial.astype(jnp.bfloat16)).astype(jnp.float32)
        column_partial = lax.optimization_barrier(column_partial.astype(jnp.bfloat16)).astype(jnp.float32)
        start = (row_index * row_span).astype(jnp.int32)
        current = lax.dynamic_slice_in_dim(row_total, start, row_span, 0)
        row_total = lax.dynamic_update_slice_in_dim(row_total, current + row_partial, start, 0)
        column_partial = column_partial.reshape(row_devices, 1, BLK_DEV, TILE, feature_count)
        current = lax.dynamic_slice_in_dim(column_total, column_index, 1, 1)
        column_total = lax.dynamic_update_slice_in_dim(column_total, current + column_partial, column_index, 1)
        return (row_total, column_total), None

    row_start = jnp.zeros((NBLK, TILE, feature_count), jnp.float32)
    column_start = jnp.zeros((row_devices, column_devices, BLK_DEV, TILE, feature_count), jnp.float32)
    (row_total, column_total), _ = lax.scan(visit_device, (row_start, column_start), (device_tiles, device_slots, device_ids))
    total = row_total.reshape(NODES, feature_count) + column_total.reshape(NODES, feature_count)
    return total.astype(jnp.bfloat16)


def reference(features, layer_weight, layer_bias, cotangent, tile_values, tile_index):
    aggregated = aggregate(features, tile_values, tile_index)
    hidden = jnp.dot(aggregated, layer_weight, preferred_element_type=jnp.float32) + layer_bias
    logistic = jax.nn.sigmoid(hidden)
    activations = (hidden * logistic).astype(jnp.bfloat16)
    derivative = logistic * (1.0 + hidden * (1.0 - logistic))
    hidden_grad = (cotangent.astype(jnp.float32) * derivative).astype(jnp.bfloat16)
    message_grad = jnp.dot(hidden_grad, layer_weight.T, preferred_element_type=jnp.float32).astype(jnp.bfloat16)
    grad_scale = NODES ** -0.5
    weight_grad = jnp.dot(aggregated.T, hidden_grad, preferred_element_type=jnp.float32) * grad_scale
    bias_grad = jnp.sum(hidden_grad.astype(jnp.float32), axis=0) * grad_scale
    node_grad = aggregate(message_grad, tile_values, tile_index)
    return activations, node_grad, weight_grad, bias_grad
```

```python
import jax
import jax.numpy as jnp
from jax import lax
from jax.experimental import pallas as pl
from jax.experimental.pallas import tpu as pltpu
from jax.sharding import Mesh
from jax.sharding import PartitionSpec as P

ROW = ("zh", "core")
COL = ("y", "x", "zl")
ALL = ROW + COL
NZ, NC, NY, NX, NL = 4, 2, 4, 4, 2
NROW, NCOL = NZ * NC, NY * NX * NL
BF16, F32 = jnp.bfloat16, jnp.float32
VMEM = pl.BlockSpec(memory_space=pltpu.VMEM)
SMEM = pl.BlockSpec(memory_space=pltpu.SMEM)


def get(value, axis, step):
    if step == 0:
        return value
    size = lax.axis_size(axis)
    return lax.ppermute(value, axis, [(i, (i - step) % size) for i in range(size)])


def put(value, axis, step):
    return get(value, axis, -step)


def column_slot(place, dz, dc):
    return lax.rem(place[0] + dz, NZ) * NC + lax.rem(place[1] + dc, NC)


def row_slot(place, dy, dx, dl):
    block = lax.rem(place[2] + dy, NY) * NX + lax.rem(place[3] + dx, NX)
    return block * NL + lax.rem(place[4] + dl, NL)


def forward_kernel(place, slots, tiles, *refs):
    inputs, outputs = refs[:8], refs[8:16]
    nodes, total = refs[16:]
    for k, ref in enumerate(inputs):
        nodes[column_slot(place, k // NC, k % NC)] = ref[...]
    for k in range(NCOL):
        total[k] = jnp.zeros(total.shape[1:], F32)

    def visit(t, carry):
        i = slots[0, t]
        j = slots[1, t]
        total[i] += jnp.dot(tiles[t], nodes[j], preferred_element_type=F32)
        return carry

    lax.fori_loop(0, place[5], visit, 0)
    for dy in range(NY):
        for dx in range(NX):
            outputs[dy][dx] = total[row_slot(place, dy, dx, 0)].astype(BF16)
            outputs[NY + dx][dy] = total[row_slot(place, dy, dx, 1)].astype(BF16)


def mirror_kernel(place, slots, tiles, *refs):
    inputs, outputs = refs[:8], refs[8:10]
    nodes, total = refs[10:]
    for dy in range(NY):
        for dx in range(NX):
            nodes[row_slot(place, dy, dx, 0)] = inputs[dy][dx]
            nodes[row_slot(place, dy, dx, 1)] = inputs[NY + dx][dy]
    for k in range(NROW):
        total[k] = jnp.zeros(total.shape[1:], F32)

    def visit(t, carry):
        i = slots[0, t]
        j = slots[1, t]
        total[j] += jnp.dot(nodes[i], tiles[t], preferred_element_type=F32)
        return carry

    lax.fori_loop(0, place[5], visit, 0)
    for dc in range(NC):
        for dz in range(NZ):
            outputs[dc][dz] = total[column_slot(place, dz, dc)].astype(BF16)


def forward_sums(place, slots, tiles, inputs):
    n, f = inputs[0].shape
    return pl.pallas_call(
        forward_kernel,
        out_shape=[jax.ShapeDtypeStruct((4, n, f), BF16)] * 8,
        in_specs=[SMEM, SMEM] + [VMEM] * 9,
        out_specs=[VMEM] * 8,
        scratch_shapes=[pltpu.VMEM((NROW, n, f), BF16), pltpu.VMEM((NCOL, n, f), F32)],
        compiler_params=pltpu.CompilerParams(vmem_limit_bytes=40 << 20),
        cost_estimate=pl.CostEstimate(
            flops=2 * 32 * n * n * f, bytes_accessed=10 << 20, transcendentals=0
        ),
    )(place, slots, tiles, *inputs)


def mirror_sums(place, slots, tiles, inputs):
    _, f, n = inputs[0].shape
    return pl.pallas_call(
        mirror_kernel,
        out_shape=[jax.ShapeDtypeStruct((4, f, n), BF16)] * 2,
        in_specs=[SMEM, SMEM] + [VMEM] * 9,
        out_specs=[VMEM] * 2,
        scratch_shapes=[pltpu.VMEM((NCOL, f, n), BF16), pltpu.VMEM((NROW, f, n), F32)],
        compiler_params=pltpu.CompilerParams(vmem_limit_bytes=40 << 20),
        cost_estimate=pl.CostEstimate(
            flops=2 * 32 * n * n * f, bytes_accessed=10 << 20, transcendentals=0
        ),
    )(place, slots, tiles, *inputs)


def column_gather(value):
    near = [get(value, "zh", dz) for dz in range(NZ)]
    return [piece for v in near for piece in (v, get(v, "core", 1))]


def row_gather(value):
    other = get(value, "zl", 1)
    a = jnp.stack([get(value, "x", dx) for dx in range(NX)])
    b = jnp.stack([get(other, "y", dy) for dy in range(NY)])
    a, b = lax.optimization_barrier((a, b))
    return [get(a, "y", dy) for dy in range(NY)] + [get(b, "x", dx) for dx in range(NX)]


def added(pieces):
    total = pieces[0].astype(F32)
    for piece in pieces[1:]:
        total += piece.astype(F32)
    return total


def row_scatter(pieces):
    a = [put(p, "y", dy) for dy, p in enumerate(pieces[:NY])]
    b = [put(p, "x", dx) for dx, p in enumerate(pieces[NY:])]
    b = [added([p[dy] for p in b]).astype(BF16) for dy in range(NY)]
    a = [added([p[dx] for p in a]).astype(BF16) for dx in range(NX)]
    b = [put(p, "y", dy) for dy, p in enumerate(b)]
    a = [put(p, "x", dx) for dx, p in enumerate(a)]
    other = put(added(b).astype(BF16), "zl", 1)
    return a + [other]


def column_scatter(pieces):
    mine, other = pieces[0], put(pieces[1], "core", 1)
    c = [added([mine[dz], other[dz]]).astype(BF16) for dz in range(NZ)]
    return [put(p, "zh", dz) for dz, p in enumerate(c)]


def aggregate_parts(place, slots, tiles, value, transposed):
    near = column_gather(value)
    far = row_gather(transposed)
    rows = row_scatter(forward_sums(place, slots, tiles, near))
    columns = column_scatter(mirror_sums(place, slots, tiles, far))
    return rows, columns


def total_of(refs):
    rows, columns = refs[:5], refs[5:9]
    return added([r[...] for r in rows]) + added([r[...] for r in columns]).T


def final_kernel(*refs):
    refs[9][...] = total_of(refs[:9]).astype(BF16)


def dense_kernel(*refs):
    weight, bias, cotangent = refs[9:12]
    aggregated_out, activations, hidden_grad_out, message, message_t = refs[12:]
    aggregated = total_of(refs[:9]).astype(BF16)
    hidden = jnp.dot(aggregated, weight[...], preferred_element_type=F32) + bias[...]
    s = jax.nn.sigmoid(hidden)
    activations[...] = (hidden * s).astype(BF16)
    derivative = s * (1.0 + hidden * (1.0 - s))
    hidden_grad = (cotangent[...].astype(F32) * derivative).astype(BF16)
    contract = (((1,), (1,)), ((), ()))
    message[...] = lax.dot_general(
        hidden_grad, weight[...], contract, preferred_element_type=F32
    ).astype(BF16)
    message_t[...] = lax.dot_general(
        weight[...], hidden_grad, contract, preferred_element_type=F32
    ).astype(BF16)
    aggregated_out[...] = aggregated
    hidden_grad_out[...] = hidden_grad


def spread(value, axes):
    return lax.all_to_all(value, axes, 0, 0, tiled=True)


def local(features, layer_weight, layer_bias, cotangent, tile_values, tile_index):
    nodes, width = features.shape
    row_index = lax.axis_index(ROW)
    block_row, block_column = tile_index[:, 0], tile_index[:, 1]
    live = jnp.sum((block_row >= 0).astype(jnp.int32))
    slots = jnp.stack([block_row - row_index * NCOL, block_column // NCOL])
    place = jnp.stack([lax.axis_index(a).astype(jnp.int32) for a in ALL] + [live])

    rows, columns = aggregate_parts(place, slots, tile_values, features, features.T)
    aggregated, activations, hidden_grad, message, message_t = pl.pallas_call(
        dense_kernel,
        out_shape=[jax.ShapeDtypeStruct((nodes, width), BF16)] * 4
        + [jax.ShapeDtypeStruct((width, nodes), BF16)],
        in_specs=[VMEM] * 12,
        out_specs=[VMEM] * 5,
    )(*rows, *columns, layer_weight, layer_bias[None], cotangent)

    rows, columns = aggregate_parts(place, slots, tile_values, message, message_t)

    scale = (nodes * NROW * NCOL) ** (-0.5)
    contract = (((0,), (0,)), ((), ()))
    weight_part = lax.dot_general(aggregated, hidden_grad, contract, preferred_element_type=F32)
    ones = jnp.ones((nodes, 128), BF16)
    bias_part = lax.dot_general(hidden_grad, ones, contract, preferred_element_type=F32)
    part = jnp.concatenate([weight_part, bias_part], axis=1) * scale
    part = part.reshape(NROW, NCOL, -1).transpose(1, 0, 2)
    part = jnp.sum(spread(part, COL), axis=0)
    part = jnp.sum(spread(part, ROW), axis=0)
    weight_grad, bias_grad = part[None, :width], part[width : width + 1]

    node_grad = pl.pallas_call(
        final_kernel,
        out_shape=jax.ShapeDtypeStruct((nodes, width), BF16),
        in_specs=[VMEM] * 9,
        out_specs=VMEM,
    )(*rows, *columns)
    return (activations, node_grad, weight_grad, bias_grad)


def solution(mesh):
    fine = Mesh(mesh.devices.reshape(NZ, NC, NY, NX, NL), ALL)
    in_specs = (
        P(ALL, None),
        P(),
        P(),
        P(ALL, None),
        P(ALL, None, None),
        P(ALL, None),
    )
    out_specs = (P(ALL, None), P(ALL, None), P(ALL, None), P(ALL))
    return jax.shard_map(local, mesh=fine, in_specs=in_specs, out_specs=out_specs, check_vma=False)
```

```python
import math

import jax
import jax.numpy as jnp
from jax import lax
from jax.experimental import pallas as pl
from jax.experimental.pallas import tpu as pltpu
from jax.sharding import Mesh
from jax.sharding import PartitionSpec as P

ROW = ("zh", "core")
COL = ("y", "x", "zl")
ALL = ROW + COL
NZ, NC, NY, NX, NL = 4, 2, 4, 4, 2
NROW, NCOL = NZ * NC, NY * NX * NL
BF16, F32 = jnp.bfloat16, jnp.float32
VMEM = pl.BlockSpec(memory_space=pltpu.VMEM)
SMEM = pl.BlockSpec(memory_space=pltpu.SMEM)
ANY = pl.BlockSpec(memory_space=pl.ANY)
CHUNKS = 4


def get(value, axis, step):
    if step == 0:
        return value
    size = lax.axis_size(axis)
    return lax.ppermute(value, axis, [(i, (i - step) % size) for i in range(size)])


def put(value, axis, step):
    return get(value, axis, -step)


def exchange(blocks, axis):
    return lax.all_to_all(blocks, axis, 0, 0, tiled=True)


def row_slot(place, first, axis_step, block_step, other):
    dy, dx = (block_step, axis_step) if first else (axis_step, block_step)
    k = lax.rem(place[2] + dy, NY) * NX + lax.rem(place[3] + dx, NX)
    return k * NL + (1 - place[4] if other else place[4])


def visit_tiles(place, tiles, held, sems, prepare, visit):
    span = held.shape[0] // CHUNKS
    parts = [pl.ds(c * span, span) for c in range(CHUNKS)]
    copies = [
        pltpu.make_async_copy(tiles.at[part], held.at[part], sems.at[c])
        for c, part in enumerate(parts)
    ]
    for copy in copies:
        copy.start()
    prepare()
    for c, copy in enumerate(copies):
        copy.wait()
        lax.fori_loop(c * span, jnp.minimum(place[5], (c + 1) * span), visit, 0)


def forward_kernel(place, slots, tiles, near, far, *refs):
    outputs, (held, sems, total) = refs[:10], refs[10:]
    core = place[1]

    def prepare():
        for k in range(NCOL):
            total[k] = jnp.zeros(total.shape[1:], F32)

    def visit(t, carry):
        i, j = slots[0, t], slots[1, t]
        z, c = lax.rem(lax.div(j, NC) + NZ - place[0], NZ), lax.rem(j, NC)

        @pl.when(c == core)
        def _():
            total[i] += jnp.dot(held[t], near[z], preferred_element_type=F32)

        @pl.when(c != core)
        def _():
            total[i] += jnp.dot(held[t], far[z], preferred_element_type=F32)

        return carry

    visit_tiles(place, tiles, held, sems, prepare, visit)
    for colour in range(2):
        own, plus, minus, more_plus, more_minus = outputs[5 * colour : 5 * colour + 5]

        def block(step, k, colour=colour):
            return total[row_slot(place, colour, step, k, colour)].astype(BF16)

        for k in range(4):
            own[k] = block(0, k)
        for k in range(2):
            plus[k] = block(2, k)
            plus[2 + k] = block(1, 2 + k)
            minus[k] = block(2, 2 + k)
            minus[2 + k] = block(3, k)
            more_plus[k] = block(1, k)
            more_minus[k] = block(3, 2 + k)


def mirror_kernel(place, slots, tiles, *refs):
    inputs, (near_out, far_out, held, sems, nodes, total) = refs[:10], refs[10:]
    core = place[1]

    def prepare():
        for colour in range(2):
            own, ahead, behind, low, high = inputs[5 * colour : 5 * colour + 5]
            for k in range(4):
                nodes[row_slot(place, colour, 0, k, colour)] = own[k]
                nodes[row_slot(place, colour, 1, k, colour)] = ahead[k]
                nodes[row_slot(place, colour, 3, k, colour)] = behind[k]
            for k in range(2):
                nodes[row_slot(place, colour, 2, k, colour)] = low[k]
                nodes[row_slot(place, colour, 2, 2 + k, colour)] = high[k]
        for k in range(NROW):
            total[k] = jnp.zeros(total.shape[1:], F32)

    def visit(t, carry):
        i, j = slots[0, t], slots[1, t]
        total[j] += jnp.dot(nodes[i], held[t], preferred_element_type=F32)
        return carry

    visit_tiles(place, tiles, held, sems, prepare, visit)
    for dz in range(NZ):
        k = lax.rem(place[0] + dz, NZ) * NC
        near_out[dz] = total[k + core].astype(BF16)
        far_out[dz] = total[k + 1 - core].astype(BF16)


def tile_sums(kernel, outs, scratch, place, slots, tiles, inputs):
    n = tiles.shape[1]
    scratch = [pltpu.VMEM(tiles.shape, tiles.dtype), pltpu.SemaphoreType.DMA((CHUNKS,)), *scratch]
    held = [m for m in scratch if m.dtype in (BF16, F32)]
    room = sum(math.prod(m.shape) * jnp.dtype(m.dtype).itemsize for m in held)
    room += 2 * (sum(map(math.prod, outs)) + sum(v.size for v in inputs))
    return pl.pallas_call(
        kernel,
        out_shape=[jax.ShapeDtypeStruct(shape, BF16) for shape in outs],
        in_specs=[SMEM, SMEM, ANY] + [VMEM] * len(inputs),
        out_specs=[VMEM] * len(outs),
        scratch_shapes=scratch,
        compiler_params=pltpu.CompilerParams(vmem_limit_bytes=(2 << 20) + room),
        cost_estimate=pl.CostEstimate(
            flops=2 * math.prod(tiles.shape) * n, bytes_accessed=10 << 20, transcendentals=0
        ),
    )(place, slots, tiles, *inputs)


def forward_sums(place, slots, tiles, near):
    n, f = tiles.shape[1], near[0].shape[-1]
    outs = [(k, n, f) for k in (4, 4, 4, 2, 2)] * 2
    return tile_sums(
        forward_kernel, outs, [pltpu.VMEM((NCOL, n, f), F32)], place, slots, tiles, near
    )


def mirror_sums(place, slots, tiles, inputs):
    n, f = tiles.shape[2], inputs[0].shape[-2]
    scratch = [pltpu.VMEM((NCOL, f, n), BF16), pltpu.VMEM((NROW, f, n), F32)]
    return tile_sums(mirror_kernel, [(NZ, f, n)] * 2, scratch, place, slots, tiles, inputs)


def column_gather(value):
    near = jnp.stack([get(value, "zh", dz) for dz in range(NZ)])
    return near, get(near, "core", 1)


def sum_of(*terms):
    total = terms[0].astype(F32)
    for term in terms[1:]:
        total += term.astype(F32)
    return total


def column_scatter(pieces):
    near, far = pieces[0], put(pieces[1], "core", 1)
    return [put(sum_of(near[dz], far[dz]).astype(BF16), "zh", dz) for dz in range(NZ)]


def aggregate_parts(place, slots, tiles, value, transposed, beside=None):
    barrier = lax.optimization_barrier
    other = get(transposed, "zl", 1)
    a = jnp.stack([get(transposed, "x", k) for k in range(NX)])
    b = jnp.stack([get(other, "y", k) for k in range(NY)])
    a, b, value, place, slots = barrier((a, b, value, place, slots))
    near = column_gather(value)
    ahead, behind = [get(a, "y", 1), get(b, "x", 1)], [get(a, "y", -1), get(b, "x", -1)]
    ahead, behind = barrier((ahead, behind))
    low = [get(behind[0][:2], "y", -1), get(behind[1][:2], "x", -1)]
    high = [get(ahead[0][2:], "y", 1), get(ahead[1][2:], "x", 1)]
    if beside is not None:
        low, high, beside = barrier((low, high, beside))
        beside = exchange(beside, ROW)
    far = [a, ahead[0], behind[0], low[0], high[0], b, ahead[1], behind[1], low[1], high[1]]

    sums = forward_sums(place, slots, tiles, near)
    half = []
    for sent, axis in ((sums[:5], "y"), (sums[5:], "x")):
        own, plus, minus, more_plus, more_minus = sent
        plus, minus = put(plus, axis, 1), put(minus, axis, -1)
        half.append((own, plus, minus, more_plus, more_minus, axis))
    done = []
    for own, plus, minus, more_plus, more_minus, axis in half:
        more_plus = put(sum_of(more_plus, plus[:2]).astype(BF16), axis, 1)
        more_minus = put(sum_of(more_minus, minus[:2]).astype(BF16), axis, -1)
        done.append(
            [sum_of(own[k], more_plus[k], minus[2 + k]).astype(BF16) for k in range(2)]
            + [sum_of(own[2 + k], plus[2 + k], more_minus[k]).astype(BF16) for k in range(2)]
        )
    columns = column_scatter(mirror_sums(place, slots, tiles, far))
    other = sum_of(*[put(p, "y", k) for k, p in enumerate(done[1])]).astype(BF16)
    rows = [put(p, "x", k) for k, p in enumerate(done[0])]
    if beside is not None:
        beside = exchange(jnp.sum(beside, axis=0)[:, None], COL)
        other, beside = barrier((other, beside))
    return [*rows, put(other, "zl", 1), *columns], beside


def total_of(refs):
    return sum_of(*[r[...] for r in refs[:5]]) + sum_of(*[r[...] for r in refs[5:9]]).T


def final_kernel(*refs):
    refs[9][...] = total_of(refs).astype(BF16)


def dense_kernel(*refs):
    weight, bias, cotangent = refs[9:12]
    aggregated_out, activations, hidden_grad_out, message, message_t = refs[12:]
    aggregated = total_of(refs).astype(BF16)
    hidden = jnp.dot(aggregated, weight[...], preferred_element_type=F32) + bias[...]
    s = jax.nn.sigmoid(hidden)
    activations[...] = (hidden * s).astype(BF16)
    derivative = s * (1.0 + hidden * (1.0 - s))
    hidden_grad = (cotangent[...].astype(F32) * derivative).astype(BF16)
    contract = (((1,), (1,)), ((), ()))
    message[...] = lax.dot_general(
        hidden_grad, weight[...], contract, preferred_element_type=F32
    ).astype(BF16)
    message_t[...] = lax.dot_general(
        weight[...], hidden_grad, contract, preferred_element_type=F32
    ).astype(BF16)
    aggregated_out[...] = aggregated
    hidden_grad_out[...] = hidden_grad


def weight_kernel(aggregated, hidden_grad, out):
    nodes, width = aggregated.shape
    scale = (nodes * NROW * NCOL) ** (-0.5)
    contract = (((0,), (0,)), ((), ()))
    ones = jnp.ones((nodes, 128), BF16)
    for k, left, right in ((0, aggregated, hidden_grad[...]), (width, hidden_grad, ones)):
        out[:, pl.ds(k, right.shape[1])] = scale * lax.dot_general(
            left[...], right, contract, preferred_element_type=F32
        )


def local(features, layer_weight, layer_bias, cotangent, tile_values, tile_index):
    nodes, width = features.shape
    row_index = lax.axis_index(ROW)
    block_row, block_column = tile_index[:, 0], tile_index[:, 1]
    live = jnp.sum((block_row >= 0).astype(jnp.int32))
    slots = jnp.stack([block_row - row_index * NCOL, block_column // NCOL])
    place = jnp.stack([lax.axis_index(a).astype(jnp.int32) for a in ALL] + [live])

    parts, _ = aggregate_parts(place, slots, tile_values, features, features.T)
    aggregated, activations, hidden_grad, message, message_t = pl.pallas_call(
        dense_kernel,
        out_shape=[jax.ShapeDtypeStruct((nodes, width), BF16)] * 4
        + [jax.ShapeDtypeStruct((width, nodes), BF16)],
        in_specs=[VMEM] * 12,
        out_specs=[VMEM] * 5,
        compiler_params=pltpu.CompilerParams(vmem_limit_bytes=6 << 20),
    )(*parts, layer_weight, layer_bias[None], cotangent)

    part = pl.pallas_call(
        weight_kernel,
        out_shape=jax.ShapeDtypeStruct((width, width + 128), F32),
        in_specs=[VMEM] * 2,
        out_specs=VMEM,
        compiler_params=pltpu.CompilerParams(vmem_limit_bytes=6 << 20),
    )(aggregated, hidden_grad)
    part = part.reshape(NROW, NCOL, -1)

    parts, part = aggregate_parts(place, slots, tile_values, message, message_t, part)
    part = jnp.sum(part, axis=(0, 1))
    weight_grad, bias_grad = part[None, :width], part[width : width + 1]

    node_grad = pl.pallas_call(
        final_kernel,
        out_shape=jax.ShapeDtypeStruct((nodes, width), BF16),
        in_specs=[VMEM] * 9,
        out_specs=VMEM,
        compiler_params=pltpu.CompilerParams(vmem_limit_bytes=6 << 20),
    )(*parts)
    return (activations, node_grad, weight_grad, bias_grad)


def solution(mesh):
    fine = Mesh(mesh.devices.reshape(NZ, NC, NY, NX, NL), ALL)
    in_specs = (
        P(ALL, None),
        P(),
        P(),
        P(ALL, None),
        P(ALL, None, None),
        P(ALL, None),
    )
    out_specs = (P(ALL, None), P(ALL, None), P(ALL, None), P(ALL))
    return jax.shard_map(local, mesh=fine, in_specs=in_specs, out_specs=out_specs, check_vma=False)
```

```python
import math

import jax
import jax.numpy as jnp
from jax import lax
from jax.experimental import pallas as pl
from jax.experimental.pallas import tpu as pltpu
from jax.sharding import Mesh
from jax.sharding import PartitionSpec as P

ROW = ("zh", "core")
COL = ("y", "x", "zl")
ALL = ROW + COL
NZ, NC, NY, NX, NL = 4, 2, 4, 4, 2
NROW, NCOL = NZ * NC, NY * NX * NL
BF16, F32 = jnp.bfloat16, jnp.float32
VMEM = pl.BlockSpec(memory_space=pltpu.VMEM)
SMEM = pl.BlockSpec(memory_space=pltpu.SMEM)
ANY = pl.BlockSpec(memory_space=pltpu.HBM)
CHUNKS = 4


def get(value, axis, step):
    if step == 0:
        return value
    size = lax.axis_size(axis)
    return lax.ppermute(value, axis, [(i, (i - step) % size) for i in range(size)])


def put(value, axis, step):
    return get(value, axis, -step)


def exchange(blocks, axis):
    return lax.all_to_all(blocks, axis, 0, 0, tiled=True)


def row_slot(place, first, axis_step, block_step, other):
    dy, dx = (block_step, axis_step) if first else (axis_step, block_step)
    k = lax.rem(place[2] + dy, NY) * NX + lax.rem(place[3] + dx, NX)
    return k * NL + (1 - place[4] if other else place[4])


def visit_tiles(place, tiles, held, sems, prepare, visit):
    span = held.shape[0] // CHUNKS
    parts = [pl.ds(c * span, span) for c in range(CHUNKS)]
    copies = [
        pltpu.make_async_copy(tiles.at[part], held.at[part], sems.at[c])
        for c, part in enumerate(parts)
    ]
    for copy in copies:
        copy.start()
    prepare()
    for c, copy in enumerate(copies):
        copy.wait()
        lax.fori_loop(c * span, jnp.minimum(place[5], (c + 1) * span), visit, 0)


def forward_kernel(place, slots, tiles, near, far, *refs):
    outputs, (held, sems, total) = refs[:10], refs[10:]
    core = place[1]

    def prepare():
        for k in range(NCOL):
            total[k] = jnp.zeros(total.shape[1:], F32)

    def visit(t, carry):
        i, j = slots[0, t], slots[1, t]
        z, c = lax.rem(lax.div(j, NC) + NZ - place[0], NZ), lax.rem(j, NC)

        @pl.when(c == core)
        def _():
            total[i] += jnp.dot(held[t], near[z], preferred_element_type=F32)

        @pl.when(c != core)
        def _():
            total[i] += jnp.dot(held[t], far[z], preferred_element_type=F32)

        return carry

    visit_tiles(place, tiles, held, sems, prepare, visit)
    for colour in range(2):
        own, plus, minus, more_plus, more_minus = outputs[5 * colour : 5 * colour + 5]

        def block(step, k, colour=colour):
            return total[row_slot(place, colour, step, k, colour)].astype(BF16)

        for k in range(4):
            own[k] = block(0, k)
        for k in range(2):
            plus[k] = block(2, k)
            plus[2 + k] = block(1, 2 + k)
            minus[k] = block(2, 2 + k)
            minus[2 + k] = block(3, k)
            more_plus[k] = block(1, k)
            more_minus[k] = block(3, 2 + k)


def mirror_kernel(place, slots, tiles, *refs):
    inputs, (near_out, far_out, held, sems, nodes, total) = refs[:10], refs[10:]
    core = place[1]

    def prepare():
        for colour in range(2):
            own, ahead, behind, low, high = inputs[5 * colour : 5 * colour + 5]
            for k in range(4):
                nodes[row_slot(place, colour, 0, k, colour)] = own[k]
                nodes[row_slot(place, colour, 1, k, colour)] = ahead[k]
                nodes[row_slot(place, colour, 3, k, colour)] = behind[k]
            for k in range(2):
                nodes[row_slot(place, colour, 2, k, colour)] = low[k]
                nodes[row_slot(place, colour, 2, 2 + k, colour)] = high[k]
        for k in range(NROW):
            total[k] = jnp.zeros(total.shape[1:], F32)

    def visit(t, carry):
        i, j = slots[0, t], slots[1, t]
        total[j] += jnp.dot(nodes[i], held[t], preferred_element_type=F32)
        return carry

    visit_tiles(place, tiles, held, sems, prepare, visit)
    for dz in range(NZ):
        k = lax.rem(place[0] + dz, NZ) * NC
        near_out[dz] = total[k + core].astype(BF16)
        far_out[dz] = total[k + 1 - core].astype(BF16)


def tile_sums(kernel, outs, scratch, place, slots, tiles, inputs):
    n = tiles.shape[1]
    scratch = [pltpu.VMEM(tiles.shape, tiles.dtype), pltpu.SemaphoreType.DMA((CHUNKS,)), *scratch]
    held = [m for m in scratch if m.dtype in (BF16, F32)]
    room = sum(math.prod(m.shape) * jnp.dtype(m.dtype).itemsize for m in held)
    room += 2 * (sum(map(math.prod, outs)) + sum(v.size for v in inputs))
    return pl.pallas_call(
        kernel,
        out_shape=[jax.ShapeDtypeStruct(shape, BF16) for shape in outs],
        in_specs=[SMEM, SMEM, ANY] + [VMEM] * len(inputs),
        out_specs=[VMEM] * len(outs),
        scratch_shapes=scratch,
        compiler_params=pltpu.CompilerParams(vmem_limit_bytes=(2 << 20) + room),
        cost_estimate=pl.CostEstimate(
            flops=2 * math.prod(tiles.shape) * n, bytes_accessed=10 << 20, transcendentals=0
        ),
    )(place, slots, pltpu.with_memory_space_constraint(tiles, pltpu.HBM), *inputs)


def forward_sums(place, slots, tiles, near):
    n, f = tiles.shape[1], near[0].shape[-1]
    outs = [(k, n, f) for k in (4, 4, 4, 2, 2)] * 2
    return tile_sums(
        forward_kernel, outs, [pltpu.VMEM((NCOL, n, f), F32)], place, slots, tiles, near
    )


def mirror_sums(place, slots, tiles, inputs):
    n, f = tiles.shape[2], inputs[0].shape[-2]
    scratch = [pltpu.VMEM((NCOL, f, n), BF16), pltpu.VMEM((NROW, f, n), F32)]
    return tile_sums(mirror_kernel, [(NZ, f, n)] * 2, scratch, place, slots, tiles, inputs)


def column_gather(value):
    near = jnp.stack([get(value, "zh", dz) for dz in range(NZ)])
    return near, get(near, "core", 1)


def sum_of(*terms):
    total = terms[0].astype(F32)
    for term in terms[1:]:
        total += term.astype(F32)
    return total


def column_scatter(pieces):
    near, far = pieces[0], put(pieces[1], "core", 1)
    return [put(sum_of(near[dz], far[dz]).astype(BF16), "zh", dz) for dz in range(NZ)]


def aggregate_parts(place, slots, tiles, value, transposed, beside=None):
    barrier = lax.optimization_barrier
    other = get(transposed, "zl", 1)
    a = jnp.stack([get(transposed, "x", k) for k in range(NX)])
    b = jnp.stack([get(other, "y", k) for k in range(NY)])
    a, b, value, place, slots = barrier((a, b, value, place, slots))
    near = column_gather(value)
    ahead, behind = [get(a, "y", 1), get(b, "x", 1)], [get(a, "y", -1), get(b, "x", -1)]
    low = [get(behind[0][:2], "y", -1), get(behind[1][:2], "x", -1)]
    high = [get(ahead[0][2:], "y", 1), get(ahead[1][2:], "x", 1)]
    if beside is not None:
        low, high, beside = barrier((low, high, beside))
        beside = exchange(beside, ROW)
    far = [a, ahead[0], behind[0], low[0], high[0], b, ahead[1], behind[1], low[1], high[1]]

    sums = forward_sums(place, slots, tiles, near)
    half = []
    for sent, axis in ((sums[:5], "y"), (sums[5:], "x")):
        own, plus, minus, more_plus, more_minus = sent
        plus, minus = put(plus, axis, 1), put(minus, axis, -1)
        half.append((own, plus, minus, more_plus, more_minus, axis))
    done = []
    for own, plus, minus, more_plus, more_minus, axis in half:
        more_plus = put(sum_of(more_plus, plus[:2]).astype(BF16), axis, 1)
        more_minus = put(sum_of(more_minus, minus[:2]).astype(BF16), axis, -1)
        done.append(
            [sum_of(own[k], more_plus[k], minus[2 + k]).astype(BF16) for k in range(2)]
            + [sum_of(own[2 + k], plus[2 + k], more_minus[k]).astype(BF16) for k in range(2)]
        )
    columns = column_scatter(mirror_sums(place, slots, tiles, far))
    other = sum_of(*[put(p, "y", k) for k, p in enumerate(done[1])]).astype(BF16)
    rows = [put(p, "x", k) for k, p in enumerate(done[0])]
    if beside is not None:
        beside = exchange(jnp.sum(beside, axis=0)[:, None], COL)
        other, beside = barrier((other, beside))
    return [*rows, put(other, "zl", 1), *columns], beside


def total_of(refs):
    return sum_of(*[r[...] for r in refs[:5]]) + sum_of(*[r[...] for r in refs[5:9]]).T


def final_kernel(*refs):
    refs[9][...] = total_of(refs).astype(BF16)


def dense_kernel(*refs):
    weight, bias, cotangent = refs[9:12]
    aggregated_out, activations, hidden_grad_out, message, message_t = refs[12:]
    aggregated = total_of(refs).astype(BF16)
    hidden = jnp.dot(aggregated, weight[...], preferred_element_type=F32) + bias[...]
    s = jax.nn.sigmoid(hidden)
    activations[...] = (hidden * s).astype(BF16)
    derivative = s * (1.0 + hidden * (1.0 - s))
    hidden_grad = (cotangent[...].astype(F32) * derivative).astype(BF16)
    contract = (((1,), (1,)), ((), ()))
    message[...] = lax.dot_general(
        hidden_grad, weight[...], contract, preferred_element_type=F32
    ).astype(BF16)
    message_t[...] = lax.dot_general(
        weight[...], hidden_grad, contract, preferred_element_type=F32
    ).astype(BF16)
    aggregated_out[...] = aggregated
    hidden_grad_out[...] = hidden_grad


def weight_kernel(aggregated, hidden_grad, out):
    nodes, width = aggregated.shape
    scale = (nodes * NROW * NCOL) ** (-0.5)
    contract = (((0,), (0,)), ((), ()))
    ones = jnp.ones((nodes, 128), BF16)
    for k, left, right in ((0, aggregated, hidden_grad[...]), (width, hidden_grad, ones)):
        out[:, pl.ds(k, right.shape[1])] = scale * lax.dot_general(
            left[...], right, contract, preferred_element_type=F32
        )


def local(features, layer_weight, layer_bias, cotangent, tile_values, tile_index):
    nodes, width = features.shape
    row_index = lax.axis_index(ROW)
    block_row, block_column = tile_index[:, 0], tile_index[:, 1]
    live = jnp.sum((block_row >= 0).astype(jnp.int32))
    slots = jnp.stack([block_row - row_index * NCOL, block_column // NCOL])
    place = jnp.stack([lax.axis_index(a).astype(jnp.int32) for a in ALL] + [live])

    parts, _ = aggregate_parts(place, slots, tile_values, features, features.T)
    aggregated, activations, hidden_grad, message, message_t = pl.pallas_call(
        dense_kernel,
        out_shape=[jax.ShapeDtypeStruct((nodes, width), BF16)] * 4
        + [jax.ShapeDtypeStruct((width, nodes), BF16)],
        in_specs=[VMEM] * 12,
        out_specs=[VMEM] * 5,
        compiler_params=pltpu.CompilerParams(vmem_limit_bytes=6 << 20),
    )(*parts, layer_weight, layer_bias[None], cotangent)

    part = pl.pallas_call(
        weight_kernel,
        out_shape=jax.ShapeDtypeStruct((width, width + 128), F32),
        in_specs=[VMEM] * 2,
        out_specs=VMEM,
        compiler_params=pltpu.CompilerParams(vmem_limit_bytes=6 << 20),
    )(aggregated, hidden_grad)
    part = part.reshape(NROW, NCOL, -1)

    parts, part = aggregate_parts(place, slots, tile_values, message, message_t, part)
    part = jnp.sum(part, axis=(0, 1))
    weight_grad, bias_grad = part[None, :width], part[width : width + 1]

    node_grad = pl.pallas_call(
        final_kernel,
        out_shape=jax.ShapeDtypeStruct((nodes, width), BF16),
        in_specs=[VMEM] * 9,
        out_specs=VMEM,
        compiler_params=pltpu.CompilerParams(vmem_limit_bytes=6 << 20),
    )(*parts)
    return (activations, node_grad, weight_grad, bias_grad)


def solution(mesh):
    fine = Mesh(mesh.devices.reshape(NZ, NC, NY, NX, NL), ALL)
    in_specs = (
        P(ALL, None),
        P(),
        P(),
        P(ALL, None),
        P(ALL, None, None),
        P(ALL, None),
    )
    out_specs = (P(ALL, None), P(ALL, None), P(ALL, None), P(ALL))
    return jax.shard_map(local, mesh=fine, in_specs=in_specs, out_specs=out_specs, check_vma=False)
```

```python
import math

import jax
import jax.numpy as jnp
from jax import lax
from jax.experimental import pallas as pl
from jax.experimental.pallas import tpu as pltpu
from jax.sharding import Mesh
from jax.sharding import PartitionSpec as P

ROW = ("zh", "core")
COL = ("y", "x", "zl")
ALL = ROW + COL
NZ, NC, NY, NX, NL = 4, 2, 4, 4, 2
NROW, NCOL = NZ * NC, NY * NX * NL
BF16, F32 = jnp.bfloat16, jnp.float32
VMEM = pl.BlockSpec(memory_space=pltpu.VMEM)
SMEM = pl.BlockSpec(memory_space=pltpu.SMEM)
ANY = pl.BlockSpec(memory_space=pltpu.HBM)
CHUNKS = 4


def get(value, axis, step):
    if step == 0:
        return value
    size = lax.axis_size(axis)
    return lax.ppermute(value, axis, [(i, (i - step) % size) for i in range(size)])


def put(value, axis, step):
    return get(value, axis, -step)


def exchange(blocks, axis):
    return lax.all_to_all(blocks, axis, 0, 0, tiled=True)


def row_slot(place, first, axis_step, block_step, other):
    dy, dx = (block_step, axis_step) if first else (axis_step, block_step)
    k = lax.rem(place[2] + dy, NY) * NX + lax.rem(place[3] + dx, NX)
    return k * NL + (1 - place[4] if other else place[4])


def visit_tiles(place, tiles, held, sems, prepare, visit):
    span = held.shape[0] // CHUNKS
    parts = [pl.ds(c * span, span) for c in range(CHUNKS)]
    copies = [
        pltpu.make_async_copy(tiles.at[part], held.at[part], sems.at[c])
        for c, part in enumerate(parts)
    ]
    for copy in copies:
        copy.start()
    prepare()
    for c, copy in enumerate(copies):
        copy.wait()
        lax.fori_loop(c * span, jnp.minimum(place[5], (c + 1) * span), visit, 0)


def forward_kernel(place, slots, tiles, near, far, *refs):
    outputs, (held, sems, total) = refs[:10], refs[10:]
    core = place[1]

    def prepare():
        for k in range(NCOL):
            total[k] = jnp.zeros(total.shape[1:], F32)

    def visit(t, carry):
        i, j = slots[0, t], slots[1, t]
        z, c = lax.rem(lax.div(j, NC) + NZ - place[0], NZ), lax.rem(j, NC)

        @pl.when(c == core)
        def _():
            total[i] += jnp.dot(held[t], near[z], preferred_element_type=F32)

        @pl.when(c != core)
        def _():
            total[i] += jnp.dot(held[t], far[z], preferred_element_type=F32)

        return carry

    visit_tiles(place, tiles, held, sems, prepare, visit)
    for colour in range(2):
        own, plus, minus, more_plus, more_minus = outputs[5 * colour : 5 * colour + 5]

        def block(step, k, colour=colour):
            return total[row_slot(place, colour, step, k, colour)].astype(BF16)

        for k in range(4):
            own[k] = block(0, k)
        for k in range(2):
            plus[k] = block(2, k)
            plus[2 + k] = block(1, 2 + k)
            minus[k] = block(2, 2 + k)
            minus[2 + k] = block(3, k)
            more_plus[k] = block(1, k)
            more_minus[k] = block(3, 2 + k)


def mirror_kernel(place, slots, tiles, *refs):
    inputs, (near_out, far_out, held, sems, nodes, total) = refs[:8], refs[8:]
    core = place[1]

    def prepare():
        for colour in range(2):
            own, ahead, behind, across = inputs[4 * colour : 4 * colour + 4]
            for k in range(4):
                nodes[row_slot(place, colour, 0, k, colour)] = own[k]
                nodes[row_slot(place, colour, 1, k, colour)] = ahead[k]
                nodes[row_slot(place, colour, 3, k, colour)] = behind[k]
                nodes[row_slot(place, colour, 2, k, colour)] = across[k]
        for k in range(NROW):
            total[k] = jnp.zeros(total.shape[1:], F32)

    def visit(t, carry):
        i, j = slots[0, t], slots[1, t]
        total[j] += jnp.dot(nodes[i], held[t], preferred_element_type=F32)
        return carry

    visit_tiles(place, tiles, held, sems, prepare, visit)
    for dz in range(NZ):
        k = lax.rem(place[0] + dz, NZ) * NC
        near_out[dz] = total[k + core].astype(BF16)
        far_out[dz] = total[k + 1 - core].astype(BF16)


def tile_sums(kernel, outs, scratch, place, slots, tiles, inputs):
    n = tiles.shape[1]
    scratch = [pltpu.VMEM(tiles.shape, tiles.dtype), pltpu.SemaphoreType.DMA((CHUNKS,)), *scratch]
    held = [m for m in scratch if m.dtype in (BF16, F32)]
    room = sum(math.prod(m.shape) * jnp.dtype(m.dtype).itemsize for m in held)
    room += 2 * (sum(map(math.prod, outs)) + sum(v.size for v in inputs))
    return pl.pallas_call(
        kernel,
        out_shape=[jax.ShapeDtypeStruct(shape, BF16) for shape in outs],
        in_specs=[SMEM, SMEM, ANY] + [VMEM] * len(inputs),
        out_specs=[VMEM] * len(outs),
        scratch_shapes=scratch,
        compiler_params=pltpu.CompilerParams(vmem_limit_bytes=(2 << 20) + room),
        cost_estimate=pl.CostEstimate(
            flops=2 * math.prod(tiles.shape) * n, bytes_accessed=10 << 20, transcendentals=0
        ),
    )(place, slots, pltpu.with_memory_space_constraint(tiles, pltpu.HBM), *inputs)


def forward_sums(place, slots, tiles, near):
    n, f = tiles.shape[1], near[0].shape[-1]
    outs = [(k, n, f) for k in (4, 4, 4, 2, 2)] * 2
    return tile_sums(
        forward_kernel, outs, [pltpu.VMEM((NCOL, n, f), F32)], place, slots, tiles, near
    )


def mirror_sums(place, slots, tiles, inputs):
    n, f = tiles.shape[2], inputs[0].shape[-2]
    scratch = [pltpu.VMEM((NCOL, f, n), BF16), pltpu.VMEM((NROW, f, n), F32)]
    return tile_sums(mirror_kernel, [(NZ, f, n)] * 2, scratch, place, slots, tiles, inputs)


def column_gather(value):
    near = jnp.stack([get(value, "zh", dz) for dz in range(NZ)])
    return near, get(near, "core", 1)


def sum_of(*terms):
    total = terms[0].astype(F32)
    for term in terms[1:]:
        total += term.astype(F32)
    return total


def column_scatter(pieces):
    near, far = pieces[0], put(pieces[1], "core", 1)
    return [put(sum_of(near[dz], far[dz]).astype(BF16), "zh", dz) for dz in range(NZ)]


def aggregate_parts(place, slots, tiles, value, transposed, beside=None):
    barrier = lax.optimization_barrier
    other = get(transposed, "zl", 1)
    a = jnp.stack([get(transposed, "x", k) for k in range(NX)])
    b = jnp.stack([get(other, "y", k) for k in range(NY)])
    a, b, value, place, slots = barrier((a, b, value, place, slots))
    near = column_gather(value)
    ahead, behind = [get(a, "y", 1), get(b, "x", 1)], [get(a, "y", -1), get(b, "x", -1)]
    across = [get(a, "y", 2), get(b, "x", 2)]
    if beside is not None:
        across, beside = barrier((across, beside))
        beside = exchange(beside, ROW)
    far = [a, ahead[0], behind[0], across[0], b, ahead[1], behind[1], across[1]]

    sums = forward_sums(place, slots, tiles, near)
    half = []
    for sent, axis in ((sums[:5], "y"), (sums[5:], "x")):
        own, plus, minus, more_plus, more_minus = sent
        plus, minus = put(plus, axis, 1), put(minus, axis, -1)
        half.append((own, plus, minus, more_plus, more_minus, axis))
    done = []
    for own, plus, minus, more_plus, more_minus, axis in half:
        more_plus = put(sum_of(more_plus, plus[:2]).astype(BF16), axis, 1)
        more_minus = put(sum_of(more_minus, minus[:2]).astype(BF16), axis, -1)
        done.append(
            [sum_of(own[k], more_plus[k], minus[2 + k]).astype(BF16) for k in range(2)]
            + [sum_of(own[2 + k], plus[2 + k], more_minus[k]).astype(BF16) for k in range(2)]
        )
    columns = column_scatter(mirror_sums(place, slots, tiles, far))
    other = sum_of(*[put(p, "y", k) for k, p in enumerate(done[1])]).astype(BF16)
    rows = [put(p, "x", k) for k, p in enumerate(done[0])]
    if beside is not None:
        beside = exchange(jnp.sum(beside, axis=0)[:, None], COL)
        other, beside = barrier((other, beside))
    return [*rows, put(other, "zl", 1), *columns], beside


def total_of(refs):
    return sum_of(*[r[...] for r in refs[:5]]) + sum_of(*[r[...] for r in refs[5:9]]).T


def final_kernel(*refs):
    refs[9][...] = total_of(refs).astype(BF16)


def dense_kernel(*refs):
    weight, bias, cotangent = refs[9:12]
    aggregated_out, activations, hidden_grad_out, message, message_t = refs[12:]
    aggregated = total_of(refs).astype(BF16)
    hidden = jnp.dot(aggregated, weight[...], preferred_element_type=F32) + bias[...]
    s = jax.nn.sigmoid(hidden)
    activations[...] = (hidden * s).astype(BF16)
    derivative = s * (1.0 + hidden * (1.0 - s))
    hidden_grad = (cotangent[...].astype(F32) * derivative).astype(BF16)
    contract = (((1,), (1,)), ((), ()))
    message[...] = lax.dot_general(
        hidden_grad, weight[...], contract, preferred_element_type=F32
    ).astype(BF16)
    message_t[...] = lax.dot_general(
        weight[...], hidden_grad, contract, preferred_element_type=F32
    ).astype(BF16)
    aggregated_out[...] = aggregated
    hidden_grad_out[...] = hidden_grad


def weight_kernel(aggregated, hidden_grad, out):
    nodes, width = aggregated.shape
    scale = (nodes * NROW * NCOL) ** (-0.5)
    contract = (((0,), (0,)), ((), ()))
    ones = jnp.ones((nodes, 128), BF16)
    for k, left, right in ((0, aggregated, hidden_grad[...]), (width, hidden_grad, ones)):
        out[:, pl.ds(k, right.shape[1])] = scale * lax.dot_general(
            left[...], right, contract, preferred_element_type=F32
        )


def local(features, layer_weight, layer_bias, cotangent, tile_values, tile_index):
    nodes, width = features.shape
    row_index = lax.axis_index(ROW)
    block_row, block_column = tile_index[:, 0], tile_index[:, 1]
    live = jnp.sum((block_row >= 0).astype(jnp.int32))
    slots = jnp.stack([block_row - row_index * NCOL, block_column // NCOL])
    place = jnp.stack([lax.axis_index(a).astype(jnp.int32) for a in ALL] + [live])

    parts, _ = aggregate_parts(place, slots, tile_values, features, features.T)
    aggregated, activations, hidden_grad, message, message_t = pl.pallas_call(
        dense_kernel,
        out_shape=[jax.ShapeDtypeStruct((nodes, width), BF16)] * 4
        + [jax.ShapeDtypeStruct((width, nodes), BF16)],
        in_specs=[VMEM] * 12,
        out_specs=[VMEM] * 5,
        compiler_params=pltpu.CompilerParams(vmem_limit_bytes=6 << 20),
    )(*parts, layer_weight, layer_bias[None], cotangent)

    part = pl.pallas_call(
        weight_kernel,
        out_shape=jax.ShapeDtypeStruct((width, width + 128), F32),
        in_specs=[VMEM] * 2,
        out_specs=VMEM,
        compiler_params=pltpu.CompilerParams(vmem_limit_bytes=6 << 20),
    )(aggregated, hidden_grad)
    part = part.reshape(NROW, NCOL, -1)

    parts, part = aggregate_parts(place, slots, tile_values, message, message_t, part)
    part = jnp.sum(part, axis=(0, 1))
    weight_grad, bias_grad = part[None, :width], part[width : width + 1]

    node_grad = pl.pallas_call(
        final_kernel,
        out_shape=jax.ShapeDtypeStruct((nodes, width), BF16),
        in_specs=[VMEM] * 9,
        out_specs=VMEM,
        compiler_params=pltpu.CompilerParams(vmem_limit_bytes=6 << 20),
    )(*parts)
    return (activations, node_grad, weight_grad, bias_grad)


def solution(mesh):
    fine = Mesh(mesh.devices.reshape(NZ, NC, NY, NX, NL), ALL)
    in_specs = (
        P(ALL, None),
        P(),
        P(),
        P(ALL, None),
        P(ALL, None, None),
        P(ALL, None),
    )
    out_specs = (P(ALL, None), P(ALL, None), P(ALL, None), P(ALL))
    return jax.shard_map(local, mesh=fine, in_specs=in_specs, out_specs=out_specs, check_vma=False)
```
